32 devices in a mesh: dp: 16 (over z, x, core), tensor: 2 (over y).
Axes of the slice: x: 2, y: 2, z: 4, core: 2. Of those that a mesh axis runs over, the one named last changes fastest.
Arguments:
- tokens: bfloat16 [16, 512, 2048], P('dp', 'tensor'), may hold values from -6 to 6
- lengths: int32 [16], P('dp'), may hold values from 1 to 512, 5120 in all
- w_query: bfloat16 [2048, 256], P('dp', 'tensor'), may hold values from -0.125 to 0.125
- w_key: bfloat16 [2048, 256], P('dp', 'tensor'), may hold values from -0.125 to 0.125
- w_value: bfloat16 [2048, 2048], P('dp', 'tensor'), may hold values from -0.125 to 0.125
- w_output: bfloat16 [2048, 2048], P('tensor', 'dp'), may hold values from -2 to 2
- gain_one: bfloat16 [2048], P('dp'), may hold values from 0.099609375 to 1.8984375
- w_gate: bfloat16 [2048, 5632], P('dp', 'tensor'), may hold values from -0.125 to 0.125
- w_up: bfloat16 [2048, 5632], P('dp', 'tensor'), may hold values from -0.125 to 0.125
- w_down: bfloat16 [5632, 2048], P('tensor', 'dp'), may hold values from -0.078125 to 0.078125
- gain_two: bfloat16 [2048], P('dp'), may hold values from 0.099609375 to 1.8984375
- cotangent: bfloat16 [16, 512, 2048], P('dp', 'tensor'), may hold values from -6 to 6
Outputs:
- outputs: bfloat16 [16, 512, 2048], P('dp', 'tensor')
- input_grad: bfloat16 [16, 512, 2048], P('dp', 'tensor')
- grad_w_query: float32 [2048, 256], P('dp', 'tensor')
- grad_w_key: float32 [2048, 256], P('dp', 'tensor')
- grad_w_value: float32 [2048, 2048], P('dp', 'tensor')
- grad_w_output: float32 [2048, 2048], P('tensor', 'dp')
- grad_gain_one: float32 [2048], P('dp')
- grad_w_gate: float32 [2048, 5632], P('dp', 'tensor')
- grad_w_up: float32 [2048, 5632], P('dp', 'tensor')
- grad_w_down: float32 [5632, 2048], P('tensor', 'dp')
- grad_gain_two: float32 [2048], P('dp')
The draws below stay inside these ranges and needn't reach their ends.
Inputs may be any that keep to these rules, and one draw needn't show every extreme that they name: `lengths`: the longest sequence fills all 512 slots.
All inputs are finite; a program needn't handle non-finite values. No bound on the sum of `lengths` on one device may be relied on, other than what follows from the above.
Results may differ from the reference program's by a relative error of at most 0.023.
Values may be sent and summed in bfloat16 or wider, within the bound.
No kernel may reach another device: no remote copies, remote signals or barrier semaphores. Data moves between devices by JAX's collectives and lax.ppermute only.
A program may use at most 192 MiB of HBM per device.

```python
import math
from functools import partial
import jax
import jax.numpy as jnp
import numpy as np
from jax import lax

D = 2048
HEADS = 16
FD = 16
HV = 128
FF = 5632
SEQ = 512
CH = 256
BATCH = 16


def spiked(values, own_key, source, target, blocks, factor):
    owner, partner = [(jnp.arange(values.shape[dim]) // (values.shape[dim] // blocks)).reshape([-1 if axis == dim else 1 for axis in range(values.ndim)]) for dim in (source, target)]
    chosen = jax.random.permutation(own_key, blocks)[partner]
    strong = (owner == chosen) | (owner == (partner + blocks // 2) % blocks)
    return jnp.where(strong, factor * values, values)


def block_scale(key, dims, pieces, least, high):
    loudness, own = 1.0, jax.random.fold_in(key, 6)
    for dim, shards_of in pieces:
        draws = jnp.exp(jax.random.uniform(jax.random.fold_in(own, dim), (shards_of,), jnp.float32, least / len(pieces), high / len(pieces)))
        loudness = loudness * jnp.repeat(draws, dims[dim] // shards_of).reshape([-1 if axis == dim else 1 for axis in range(len(dims))])
    return loudness


def length_profile(number_of, total, limit, lean):
    loads = [(1 << 20) // math.isqrt(grade ** lean) + 1 for grade in range(2, number_of + 1)]
    surplus, holding = total - limit - (number_of - 1), [1] * (number_of - 1)
    while surplus > 0:
        movable = [i for i in range(number_of - 1) if holding[i] < limit]
        pool, budget = sum([loads[i] for i in movable]), surplus
        for i in movable:
            extra = min(limit - holding[i], max(1, budget * loads[i] // pool), surplus)
            holding[i] = holding[i] + extra
            surplus = surplus - extra
    return np.array([limit] + holding)


def ragged(own_key, number_of, total, reach, slope):
    if number_of == 2:
        one = jax.random.randint(own_key, (), max(1, total - reach), min(reach, total - 1) + 1)
        return jnp.stack([one, total - one])
    sizes = jnp.asarray(length_profile(number_of, total, reach, slope), jnp.int32)
    couples = (number_of - 1) // 2
    giver, sink = sizes[1:1 + 2 * couples:2], sizes[2:2 + 2 * couples:2]
    slack = jnp.minimum(giver - 1, reach - sink)
    shifted = jax.random.randint(jax.random.fold_in(own_key, 1), (couples,), 0, 1 << 20) % (slack + 1)
    sizes = sizes.at[1:1 + 2 * couples:2].set(giver - shifted).at[2:2 + 2 * couples:2].set(sink + shifted)
    return sizes[jax.random.permutation(jax.random.fold_in(own_key, 2), number_of)]


def gaussian(stream_key, shape, width, reach, cuts=(), kind=jnp.bfloat16):
    entries = width * jax.random.normal(stream_key, shape, jnp.float32)
    if cuts:
        entries = entries * block_scale(stream_key, shape, cuts, -0.22, 0.18)
    return jnp.clip(entries, -reach, reach).astype(kind)


def noise_with(key, shape, width, limit, split, heavy, kind=jnp.bfloat16):
    drawn = width * jax.random.normal(key, shape, jnp.float32)
    if split:
        drawn = drawn * block_scale(key, shape, split, -0.22, 0.18)
    return jnp.clip(spiked(drawn, jax.random.fold_in(key, 3), *heavy), -limit, limit).astype(kind)


def setup_inputs(seed: int = 0) -> dict:
    streams_of = jax.random.split(jax.random.key(seed), 13)
    return {
        "tokens": noise_with(streams_of[0], (BATCH, SEQ, D), 1.0, 6.0, ((0, 16), (1, 2)), (0, 2, 16, 2.0)),
        "lengths": ragged(streams_of[1], BATCH, BATCH * SEQ * 5 // 8, SEQ, 1).astype(jnp.int32),
        "w_query": gaussian(streams_of[2], (D, HEADS * FD), D ** -0.5, 0.125, ((0, 16), (1, 2))),
        "w_key": gaussian(streams_of[3], (D, HEADS * FD), D ** -0.5, 0.125, ((0, 16), (1, 2))),
        "w_value": gaussian(streams_of[4], (D, HEADS * HV), D ** -0.5, 0.125, ((0, 16), (1, 2))),
        "w_output": gaussian(streams_of[5], (HEADS * HV, D), (max(HEADS * HV // 256, 1)) ** -0.5, 2.0, ((0, 2), (1, 16))),
        "gain_one": jnp.clip(1.0 + 0.18 * jax.random.normal(streams_of[6], (D,), jnp.float32), 0.099609375, 1.8984375).astype(jnp.bfloat16),
        "w_gate": gaussian(streams_of[7], (D, FF), D ** -0.5, 0.125, ((0, 16), (1, 2))),
        "w_up": gaussian(streams_of[8], (D, FF), D ** -0.5, 0.125, ((0, 16), (1, 2))),
        "w_down": gaussian(streams_of[9], (FF, D), FF ** -0.5, 0.078125, ((0, 2), (1, 16))),
        "gain_two": jnp.clip(1.0 + 0.18 * jax.random.normal(streams_of[10], (D,), jnp.float32), 0.099609375, 1.8984375).astype(jnp.bfloat16),
        "cotangent": noise_with(streams_of[11], (BATCH, SEQ, D), 1.0, 6.0, ((0, 16), (1, 2)), (0, 2, 16, 2.0)),
    }


epsilon = 1e-05
top_precision = lax.Precision.HIGHEST

@jax.custom_vjp
def low(v):
    return lax.optimization_barrier(v.astype(jnp.bfloat16)).astype(jnp.float32)

@jax.custom_vjp
def low_back(v):
    return v

def low_keep(v):
    return (low(v), None)

def low_pass(kept, grad):
    return (grad,)

def back_keep(v):
    return (v, None)

def back_low(kept, grad):
    return (low(grad),)
low.defvjp(low_keep, low_pass)
low_back.defvjp(back_keep, back_low)

def rms_scale(value_rows):
    return lax.rsqrt(lax.optimization_barrier(jnp.mean(value_rows * value_rows, axis=-1, keepdims=True)) + epsilon)

def normalize(value_rows, gain_vec):
    return value_rows * rms_scale(value_rows) * gain_vec

def feature_map(vectors):
    feat_width = vectors.shape[-1]
    outer_prod = (vectors[..., :, None] * vectors[..., None, :]).reshape(vectors.shape[:-1] + (feat_width * feat_width,))
    ones_col = jnp.ones(vectors.shape[:-1] + (1,), jnp.float32)
    return jnp.concatenate([ones_col, vectors * feat_width ** (-0.25), outer_prod * (0.5 / feat_width) ** 0.5], axis=-1)

def block_step(carried, block_in):
    running_state, normal = carried
    queries, keys_in, value_rows = block_in
    feat_width = queries.shape[-1]
    scores = jnp.einsum('hqf,hkf->hqk', queries, keys_in, precision=top_precision) * feat_width ** (-0.5)
    row_index = lax.broadcasted_iota(jnp.int32, scores.shape, 1)
    col_index = lax.broadcasted_iota(jnp.int32, scores.shape, 2)
    layer_routine = jnp.where(row_index >= col_index, 1.0 + scores + 0.5 * scores * scores, 0.0)
    query_taylor_map = feature_map(queries)
    key_taylor_map = feature_map(keys_in)
    attention_numer = jnp.einsum('atn,anx->atx', layer_routine, value_rows, precision=top_precision) + jnp.einsum('pxo,poi->pxi', query_taylor_map, running_state, precision=top_precision)
    denominator = lax.optimization_barrier(jnp.sum(layer_routine, axis=-1)) + jnp.einsum('hqf,hf->hq', query_taylor_map, normal, precision=top_precision)
    outputs = attention_numer / denominator[..., None]
    updated_state = running_state + jnp.einsum('alb,alx->abx', key_taylor_map, value_rows, precision=top_precision)
    next_normal = normal + lax.optimization_barrier(jnp.sum(key_taylor_map, axis=1))
    return ((updated_state, next_normal), outputs)

def attend(queries, keys_in, value_rows, head_count, block_len, key_width, value_width):
    row_total = queries.shape[0]
    blocks = row_total // block_len
    feat_count = 1 + key_width + key_width * key_width

    def to_blocks(flat_array, last_width):
        return flat_array.reshape(blocks, block_len, head_count, last_width).transpose(0, 2, 1, 3)
    initial = (jnp.zeros((head_count, feat_count, value_width), jnp.float32), jnp.zeros((head_count, feat_count), jnp.float32))
    final_carry, outputs = lax.scan(jax.checkpoint(block_step), initial, (to_blocks(queries, key_width), to_blocks(keys_in, key_width), to_blocks(value_rows, value_width)))
    return outputs.transpose(0, 2, 1, 3).reshape(row_total, head_count * value_width)

def block_layer(mask_col, inputs, w_query, w_key, w_value, w_output, gain_one, w_gate, w_up, w_down, gain_two):
    masked = inputs * mask_col
    normed = low(normalize(masked, gain_one))
    queries = low(low_back(jnp.dot(normed, w_query, precision=top_precision)))
    keys_in = low(low_back(jnp.dot(normed, w_key, precision=top_precision)))
    value_rows = low(low_back(jnp.dot(normed, w_value, precision=top_precision)))
    mixed = low(attend(queries, keys_in, value_rows, HEADS, CH, FD, HV))
    branch = low_back(jnp.dot(mixed, w_output, precision=top_precision))
    hidden = masked + branch
    normed_two = low(normalize(hidden, gain_two))
    gate_val = low_back(jnp.dot(normed_two, w_gate, precision=top_precision))
    upward = low_back(jnp.dot(normed_two, w_up, precision=top_precision))
    activation = low(jax.nn.silu(gate_val) * upward)
    feed_out = low_back(jnp.dot(activation, w_down, precision=top_precision))
    return (hidden + feed_out) * mask_col

def reference(tokens, lengths, w_query, w_key, w_value, w_output, gain_one, w_gate, w_up, w_down, gain_two, cotangent):
    weights = tuple((weight.astype(jnp.float32) for weight in (w_query, w_key, w_value, w_output, gain_one, w_gate, w_up, w_down, gain_two)))
    positions = jnp.arange(SEQ, dtype=jnp.int32)

    def per_sequence(totals, item_in):
        row_in, length_val, row_cot = item_in
        mask_col = (positions < length_val).astype(jnp.float32)[:, None]
        result, pullback = jax.vjp(partial(block_layer, mask_col), row_in.astype(jnp.float32), *weights)
        grads = pullback(row_cot.astype(jnp.float32))
        new_totals = tuple((summed + added for summed, added in zip(totals, grads[1:])))
        return (new_totals, (result.astype(jnp.bfloat16), grads[0].astype(jnp.bfloat16)))
    initial = tuple((jnp.zeros(weight.shape, jnp.float32) for weight in weights))
    totals, (outputs, input_grad) = lax.scan(per_sequence, initial, (tokens, lengths, cotangent))
    return (outputs, input_grad, totals[0], totals[1], totals[2], totals[3], totals[4], totals[5], totals[6], totals[7], totals[8])
```

```python
import jax
import jax.numpy as jnp
from jax import lax
from jax.experimental import pallas as pl
from jax.experimental.pallas import tpu as pltpu
from jax.sharding import Mesh, PartitionSpec as P

FD = 16
HV = 128
EPS = 1e-05
SWAP = [(0, 1), (1, 0)]
F32 = jnp.float32
BF16 = jnp.bfloat16


def dot(left, right, left_dim, right_dim):
    return lax.dot_general(
        left, right, (((left_dim,), (right_dim,)), ((), ())), preferred_element_type=F32
    )


def gather_rows(block):
    rows = block.shape[0]
    from_x = lax.ppermute(block, "x", SWAP)
    from_t = lax.ppermute(block, "t", SWAP)
    upper = lax.ppermute(from_t[: rows // 2], "x", SWAP)
    lower = lax.ppermute(from_x[rows // 2 :], "t", SWAP)
    near = jnp.concatenate([block, from_t, from_x, upper, lower], axis=0)
    far = lax.ppermute(near, "c", SWAP)
    return jnp.concatenate([near, far], axis=0)


def add(left, right):
    return (left.astype(F32) + right.astype(F32)).astype(BF16)


def scatter_rows(partial):
    total = partial.shape[0]
    here = add(partial[: total // 2], lax.ppermute(partial[total // 2 :], "c", SWAP))
    rows = total // 8
    half = rows // 2
    tops = [here[i * rows : i * rows + half] for i in range(4)]
    ends = [here[i * rows + half : (i + 1) * rows] for i in range(4)]
    got_x = lax.ppermute(jnp.concatenate([tops[2], tops[3]], axis=0), "x", SWAP)
    got_t = lax.ppermute(jnp.concatenate([ends[1], ends[3]], axis=0), "t", SWAP)
    last_t = lax.ppermute(add(tops[1], got_x[half:]), "t", SWAP)
    last_x = lax.ppermute(add(ends[2], got_t[half:]), "x", SWAP)
    top = tops[0].astype(F32) + got_x[:half].astype(F32) + last_t.astype(F32)
    end = ends[0].astype(F32) + got_t[:half].astype(F32) + last_x.astype(F32)
    return jnp.concatenate([top, end], axis=0)


def pick(array, axis, index):
    return lax.dynamic_index_in_dim(array, index, axis, keepdims=False)


def trade(array, split, join, axis_name):
    me = lax.axis_index(axis_name)
    kept = pick(array, split, me)
    got = lax.ppermute(pick(array, split, 1 - me), axis_name, SWAP)
    kept = jnp.expand_dims(kept, join)
    got = jnp.expand_dims(got, join)
    return jnp.where(
        me == 0,
        jnp.concatenate([kept, got], axis=join),
        jnp.concatenate([got, kept], axis=join),
    )


def inward_rows(weight):
    d, _, n = weight.shape
    step = trade(weight.reshape(d, 2, 2, n), 2, 0, "c")
    step = trade(step, 2, 0, "x")
    return step.reshape(4 * d, n)


def outward_rows(grad):
    d, n = grad.shape[0] // 4, grad.shape[1]
    step = trade(grad.reshape(2, 2, d, n), 0, 2, "x")
    step = trade(step, 0, 2, "c")
    return step.reshape(d, 4, n)


def inward_cols(weight):
    _, n, d = weight.shape
    step = trade(weight.reshape(2, 2, n, d), 1, 2, "c")
    step = trade(step, 0, 1, "x")
    return step.reshape(n, 4 * d)


def outward_cols(grad):
    n, d = grad.shape[0], grad.shape[1] // 4
    step = trade(grad.reshape(n, 2, 2, d), 1, 0, "x")
    step = trade(step, 2, 1, "c")
    return step.reshape(4, n, d)


def lanes_of(head, rows):
    lane = lax.broadcasted_iota(jnp.int32, (rows, 128), 1)
    return (lane >= head * FD) & (lane < (head + 1) * FD)


def head_parts(proj_ref, start, rows, heads):
    tile = proj_ref[pl.ds(start, rows), heads * HV :].astype(F32)
    keys = pltpu.roll(tile, 128 - heads * FD, 1)
    return tile, keys.astype(BF16)


def forward_kernel(half_ref, u_ref, w_ref, wo_ref, part_ref, proj_ref, mixed_ref, scale_ref):
    heads = wo_ref.shape[0] // HV
    size = u_ref.shape[0]
    rows = size // 2
    tokens = u_ref[...]
    wide = tokens.astype(F32)
    scale = lax.rsqrt(jnp.mean(wide * wide, axis=-1, keepdims=True) + EPS)
    scale_ref[...] = jnp.broadcast_to(scale, (size, 128))
    proj_ref[...] = (dot(tokens, w_ref[...], 1, 0) * scale).astype(BF16)
    first = pl.multiple_of(half_ref[0] * rows, rows)
    second = pl.multiple_of(rows - half_ref[0] * rows, rows)
    tile_a, keys_a = head_parts(proj_ref, first, rows, heads)
    tile_b, keys_b = head_parts(proj_ref, second, rows, heads)
    causal = lax.broadcasted_iota(jnp.int32, (rows, rows), 0) >= lax.broadcasted_iota(
        jnp.int32, (rows, rows), 1
    )

    def taylor(queries, keys):
        score = dot(queries, keys, 1, 1) * (FD**-0.5)
        return 1.0 + score + 0.5 * score * score

    for head in range(heads):
        here = lanes_of(head, rows)
        cols = slice(head * HV, (head + 1) * HV)
        query_a = jnp.where(here, tile_a, 0.0).astype(BF16)
        query_b = jnp.where(here, tile_b, 0.0).astype(BF16)
        value_a = proj_ref[pl.ds(first, rows), cols]
        value_b = proj_ref[pl.ds(second, rows), cols]
        aa = jnp.where(causal, taylor(query_a, keys_a), 0.0)
        bb = jnp.where(causal, taylor(query_b, keys_b), 0.0)
        ba = taylor(query_b, keys_a)
        den_a = jnp.sum(aa, axis=-1, keepdims=True)
        den_b = jnp.sum(bb, axis=-1, keepdims=True) + jnp.sum(ba, axis=-1, keepdims=True)
        out_a = dot(aa.astype(BF16), value_a, 1, 0) / den_a
        out_b = (dot(ba.astype(BF16), value_a, 1, 0) + dot(bb.astype(BF16), value_b, 1, 0)) / den_b
        mixed_ref[pl.ds(first, rows), cols] = out_a.astype(BF16)
        mixed_ref[pl.ds(second, rows), cols] = out_b.astype(BF16)
    part_ref[...] = dot(mixed_ref[...], wo_ref[...], 1, 0).astype(BF16)


def backward_kernel(
    half_ref, back_ref, u_ref, w_ref, wo_ref, proj_ref, mixed_ref, scale_ref,
    part_ref, grad_w_ref, grad_wo_ref, inner_ref, delta_ref, acc_w_ref, acc_wo_ref,
):
    heads = wo_ref.shape[0] // HV
    size = u_ref.shape[0]
    rows = size // 2
    step = pl.program_id(0)
    inner_ref[...] = dot(back_ref[...], wo_ref[...], 1, 1)
    first = pl.multiple_of(half_ref[0] * rows, rows)
    second = pl.multiple_of(rows - half_ref[0] * rows, rows)
    tile_a, keys_a = head_parts(proj_ref, first, rows, heads)
    tile_b, keys_b = head_parts(proj_ref, second, rows, heads)
    causal = lax.broadcasted_iota(jnp.int32, (rows, rows), 0) >= lax.broadcasted_iota(
        jnp.int32, (rows, rows), 1
    )
    scale_a = scale_ref[pl.ds(first, rows), :]
    scale_b = scale_ref[pl.ds(second, rows), :]
    zero = jnp.zeros((rows, 128), F32)
    query_back_a, query_back_b, key_back_a, key_back_b = zero, zero, zero, zero

    def score_of(queries, keys):
        return dot(queries, keys, 1, 1) * (FD**-0.5)

    for head in range(heads):
        here = lanes_of(head, rows)
        cols = slice(head * HV, (head + 1) * HV)
        query_a = jnp.where(here, tile_a, 0.0).astype(BF16)
        query_b = jnp.where(here, tile_b, 0.0).astype(BF16)
        value_a = proj_ref[pl.ds(first, rows), cols]
        value_b = proj_ref[pl.ds(second, rows), cols]
        s_aa, s_bb, s_ba = (
            score_of(query_a, keys_a),
            score_of(query_b, keys_b),
            score_of(query_b, keys_a),
        )
        k_aa = jnp.where(causal, 1.0 + s_aa + 0.5 * s_aa * s_aa, 0.0)
        k_bb = jnp.where(causal, 1.0 + s_bb + 0.5 * s_bb * s_bb, 0.0)
        k_ba = 1.0 + s_ba + 0.5 * s_ba * s_ba
        inv_a = 1.0 / jnp.sum(k_aa, axis=-1, keepdims=True)
        inv_b = 1.0 / (jnp.sum(k_bb, axis=-1, keepdims=True) + jnp.sum(k_ba, axis=-1, keepdims=True))
        g_a = inner_ref[pl.ds(first, rows), cols] * inv_a
        g_b = inner_ref[pl.ds(second, rows), cols] * inv_b
        c_a = -jnp.sum(g_a * mixed_ref[pl.ds(first, rows), cols].astype(F32), axis=-1, keepdims=True)
        c_b = -jnp.sum(g_b * mixed_ref[pl.ds(second, rows), cols].astype(F32), axis=-1, keepdims=True)
        g_a, g_b = g_a.astype(BF16), g_b.astype(BF16)
        value_back_a = dot(k_aa.astype(BF16), g_a, 0, 0) + dot(k_ba.astype(BF16), g_b, 0, 0)
        value_back_b = dot(k_bb.astype(BF16), g_b, 0, 0)
        delta_ref[pl.ds(first, rows), cols] = (value_back_a * scale_a).astype(BF16)
        delta_ref[pl.ds(second, rows), cols] = (value_back_b * scale_b).astype(BF16)
        d_aa = jnp.where(causal, (dot(g_a, value_a, 1, 1) + c_a) * (1.0 + s_aa), 0.0).astype(BF16)
        d_bb = jnp.where(causal, (dot(g_b, value_b, 1, 1) + c_b) * (1.0 + s_bb), 0.0).astype(BF16)
        d_ba = ((dot(g_b, value_a, 1, 1) + c_b) * (1.0 + s_ba)).astype(BF16)
        query_back_a += jnp.where(here, dot(d_aa, keys_a, 1, 0), 0.0)
        query_back_b += jnp.where(here, dot(d_bb, keys_b, 1, 0) + dot(d_ba, keys_a, 1, 0), 0.0)
        key_back_a += dot(d_aa, query_a, 0, 0) + dot(d_ba, query_b, 0, 0)
        key_back_b += dot(d_bb, query_b, 0, 0)
    shift = heads * FD
    tail = slice(heads * HV, heads * HV + 128)
    tile_back_a = (query_back_a + pltpu.roll(key_back_a, shift, 1)) * (scale_a * FD**-0.5)
    tile_back_b = (query_back_b + pltpu.roll(key_back_b, shift, 1)) * (scale_b * FD**-0.5)
    delta_ref[pl.ds(first, rows), tail] = tile_back_a.astype(BF16)
    delta_ref[pl.ds(second, rows), tail] = tile_back_b.astype(BF16)
    delta = delta_ref[...]
    part_ref[...] = dot(delta, w_ref[...], 1, 1).astype(BF16)

    @pl.when(step == 0)
    def _():
        acc_w_ref[...] = jnp.zeros_like(acc_w_ref)
        acc_wo_ref[...] = jnp.zeros_like(acc_wo_ref)

    acc_w_ref[...] += dot(u_ref[...], delta, 0, 0)
    acc_wo_ref[...] += dot(mixed_ref[...], back_ref[...], 0, 0)

    @pl.when(step == pl.num_programs(0) - 1)
    def _():
        grad_w_ref[...] = acc_w_ref[...].astype(BF16)
        grad_wo_ref[...] = acc_wo_ref[...].astype(BF16)


def attention(half, tokens, w_in, w_out, size):
    total, width = tokens.shape
    columns, inner = w_in.shape[1], w_out.shape[0]
    by_seq = lambda n: pl.BlockSpec((size, n), lambda i, half: (i, 0))
    whole = lambda a: pl.BlockSpec(a.shape, lambda i, half: (0, 0))
    return pl.pallas_call(
        forward_kernel,
        out_shape=(
            jax.ShapeDtypeStruct((total, width), BF16),
            jax.ShapeDtypeStruct((total, columns), BF16),
            jax.ShapeDtypeStruct((total, inner), BF16),
            jax.ShapeDtypeStruct((total, 128), F32),
        ),
        grid_spec=pltpu.PrefetchScalarGridSpec(
            num_scalar_prefetch=1,
            grid=(total // size,),
            in_specs=[by_seq(width), whole(w_in), whole(w_out)],
            out_specs=[by_seq(width), by_seq(columns), by_seq(inner), by_seq(128)],
        ),
        compiler_params=pltpu.CompilerParams(vmem_limit_bytes=40 << 20),
        cost_estimate=pl.CostEstimate(
            flops=2 * total * width * (columns + inner) + 8 * total * size * inner,
            bytes_accessed=4 * total * width + 4 * total * columns,
            transcendentals=total,
        ),
    )(half, tokens, w_in, w_out)


def attention_back(half, back, tokens, w_in, w_out, proj, mixed, scale, size):
    total, width = tokens.shape
    columns, inner = w_in.shape[1], w_out.shape[0]
    by_seq = lambda n: pl.BlockSpec((size, n), lambda i, half: (i, 0))
    whole = lambda a: pl.BlockSpec(a.shape, lambda i, half: (0, 0))
    return pl.pallas_call(
        backward_kernel,
        out_shape=(
            jax.ShapeDtypeStruct((total, width), BF16),
            jax.ShapeDtypeStruct(w_in.shape, BF16),
            jax.ShapeDtypeStruct(w_out.shape, BF16),
        ),
        grid_spec=pltpu.PrefetchScalarGridSpec(
            num_scalar_prefetch=1,
            grid=(total // size,),
            in_specs=[
                by_seq(width), by_seq(width), whole(w_in), whole(w_out),
                by_seq(columns), by_seq(inner), by_seq(128),
            ],
            out_specs=[by_seq(width), whole(w_in), whole(w_out)],
            scratch_shapes=[
                pltpu.VMEM((size, inner), F32),
                pltpu.VMEM((size, columns), BF16),
                pltpu.VMEM(w_in.shape, F32),
                pltpu.VMEM(w_out.shape, F32),
            ],
        ),
        compiler_params=pltpu.CompilerParams(vmem_limit_bytes=48 << 20),
        cost_estimate=pl.CostEstimate(
            flops=4 * total * width * (columns + inner) + 24 * total * size * inner,
            bytes_accessed=6 * total * width + 4 * total * columns,
            transcendentals=total,
        ),
    )(half, back, tokens, w_in, w_out, proj, mixed, scale)


def per_device(
    tokens, lengths, w_query, w_key, w_value, w_output, gain_one,
    w_gate, w_up, w_down, gain_two, cotangent,
):
    local_rows, width = tokens.shape[1:]
    shard = w_query.shape[0]
    heads = w_query.shape[1] // FD // 4
    hidden_units = w_gate.shape[1] // 4
    half = lax.axis_index("t")
    position = half * local_rows + lax.iota(jnp.int32, local_rows)
    mask = (position < lengths[0]).astype(F32)[:, None]
    half_index = jnp.reshape(half, (1,)).astype(jnp.int32)

    scale_one = gain_one.astype(F32)[:, None, None]
    parts = jnp.concatenate(
        [
            w_value.reshape(shard, 4, heads * HV),
            w_query.reshape(shard, 4, heads * FD),
            w_key.reshape(shard, 4, heads * FD),
        ],
        axis=2,
    )
    own_in = parts.astype(F32)
    w_in = (own_in * scale_one).astype(BF16)
    w_in = jnp.pad(w_in, ((0, 0), (0, 0), (0, 128 - 2 * heads * FD)))
    w_in = lax.all_gather(inward_rows(w_in), "g", axis=0, tiled=True)
    w_out = inward_cols(w_output.reshape(4, heads * HV, shard))
    w_out = lax.all_gather(w_out, "g", axis=1, tiled=True)

    own = (tokens[0].astype(F32) * mask).astype(BF16)
    all_tokens = gather_rows(own)

    scale_two = gain_two.astype(F32)[:, None, None]
    own_gate = w_gate.reshape(shard, 4, hidden_units).astype(F32)
    own_up = w_up.reshape(shard, 4, hidden_units).astype(F32)
    gate_w = inward_rows((own_gate * scale_two).astype(BF16))
    up_w = inward_rows((own_up * scale_two).astype(BF16))
    down_w = inward_cols(w_down.reshape(4, hidden_units, shard))
    gate_w = lax.all_gather(gate_w, "g", axis=0, tiled=True)
    up_w = lax.all_gather(up_w, "g", axis=0, tiled=True)
    down_w = lax.all_gather(down_w, "g", axis=1, tiled=True)

    size = 2 * local_rows
    part, proj, mixed, scale = attention(half_index, all_tokens, w_in, w_out, size)
    hidden = own.astype(F32) + scatter_rows(part)
    r_two = lax.rsqrt(jnp.mean(hidden * hidden, axis=-1, keepdims=True) + EPS)
    normed = gather_rows((hidden * r_two).astype(BF16))
    gate = dot(normed, gate_w, 1, 0)
    upward = dot(normed, up_w, 1, 0)
    sig = jax.nn.sigmoid(gate)
    silu = gate * sig
    activation = (silu * upward).astype(BF16)
    feed = scatter_rows(dot(activation, down_w, 1, 0).astype(BF16))
    result = ((hidden + feed) * mask).astype(BF16)[None]

    out_back = cotangent[0].astype(F32) * mask
    feed_back = gather_rows(out_back.astype(BF16))
    grad_down = dot(activation, feed_back, 0, 0).astype(BF16)
    act_back = dot(feed_back, down_w, 1, 1)
    up_back = (act_back * silu).astype(BF16)
    gate_back = (act_back * upward * sig * (1.0 + gate * (1.0 - sig))).astype(BF16)
    grad_gate = dot(normed, gate_back, 0, 0).astype(BF16)
    grad_up = dot(normed, up_back, 0, 0).astype(BF16)
    y_two = scatter_rows((dot(gate_back, gate_w, 1, 1) + dot(up_back, up_w, 1, 1)).astype(BF16))
    hidden_back = (
        out_back
        + r_two * y_two
        - hidden * (r_two**3 * jnp.mean(y_two * hidden, axis=-1, keepdims=True))
    )
    branch_back = gather_rows(hidden_back.astype(BF16))
    part, grad_in, grad_out = attention_back(
        half_index, branch_back, all_tokens, w_in, w_out, proj, mixed, scale, size
    )
    y_one = scatter_rows(part)
    wide = own.astype(F32)
    r_sq = 1.0 / (jnp.mean(wide * wide, axis=-1, keepdims=True) + EPS)
    masked_back = y_one - wide * (r_sq * jnp.mean(y_one * wide, axis=-1, keepdims=True))
    input_grad = ((hidden_back + masked_back) * mask).astype(BF16)[None]

    def rows_of(grad):
        return outward_rows(lax.psum_scatter(grad, "g", scatter_dimension=0, tiled=True)).astype(F32)

    def cols_of(grad):
        out = outward_cols(lax.psum_scatter(grad, "g", scatter_dimension=1, tiled=True))
        return out.reshape(-1, shard).astype(F32)

    grad_down = cols_of(grad_down)
    grad_gate = rows_of(grad_gate)
    grad_up = rows_of(grad_up)
    grad_out = cols_of(grad_out)
    grad_in = rows_of(grad_in)[:, :, : own_in.shape[2]]
    sum_one = jnp.sum(own_in * grad_in, axis=(1, 2))
    sum_two = jnp.sum(own_gate * grad_gate + own_up * grad_up, axis=(1, 2))
    sums = jnp.stack([sum_one, sum_two])
    sums = sums + lax.ppermute(sums, "t", SWAP)
    grad_in = grad_in * scale_one
    wide_v, wide_qk = heads * HV, heads * FD
    return (
        result,
        input_grad,
        grad_in[:, :, wide_v : wide_v + wide_qk].reshape(shard, -1),
        grad_in[:, :, wide_v + wide_qk :].reshape(shard, -1),
        grad_in[:, :, :wide_v].reshape(shard, -1),
        grad_out,
        sums[0],
        (grad_gate * scale_two).reshape(shard, -1),
        (grad_up * scale_two).reshape(shard, -1),
        grad_down,
        sums[1],
    )


def solution(mesh):
    groups = mesh.shape["dp"] // 4
    grid = Mesh(mesh.devices.reshape(groups, 2, 2, mesh.shape["tensor"]), ("g", "x", "c", "t"))
    dp = ("g", "x", "c")
    tokens, rows, cols, vector = P(dp, "t", None), P(dp, "t"), P("t", dp), P(dp)
    return jax.shard_map(
        per_device,
        mesh=grid,
        in_specs=(
            tokens, vector, rows, rows, rows, cols, vector, rows, rows, cols, vector, tokens,
        ),
        out_specs=(
            tokens, tokens, rows, rows, rows, cols, vector, rows, rows, cols, vector,
        ),
        check_vma=False,
    )
```
